256 devices in a mesh: samp: 8 (over x, core), var: 32 (over z, y).
Axes of the slice: x: 4, y: 4, z: 8, core: 2. Of those that a mesh axis runs over, the one named last changes fastest.
Arguments:
- phenotype: bfloat16 [65536, 256], P(('samp', 'var')), may hold values from -1500 to 1500
- inverse_blocks: float32 [256, 256, 256], P(('samp', 'var')), may hold values from -1 to 2, as said below
- bin_sizes: int32 [8, 32], P('samp', 'var'), may hold values from 128 to 256, as said below
- slot_of: int32 [49152], P('samp'), may hold values from 0 to 8191, as said below
- dosages: bfloat16 [49152, 32768], P('samp', 'var'), may hold values from 0 to 2
Outputs:
- z_scores: float32 [32768, 256], P('var', 'samp')
The draws below stay inside these ranges and needn't reach their ends.
Inputs may be any that keep to these rules, and one draw needn't show every extreme that they name: `bin_sizes`: within each row (one sample shard) the sizes sum to 192 times the row's length, and at least one bin is full. `slot_of`: within each sample shard the samples occupy exactly the live slots: slot v * 256 + r with r < bin_sizes of bin v, each once. `inverse_blocks`: each block is symmetric positive definite.
All inputs are finite; a program needn't handle non-finite values.
Results may differ from the reference program's by a relative error of at most 0.0041.
Values may be sent and summed in bfloat16 or wider, within the bound.
A program may use at most 128 MiB of HBM per device.

```python
import math
import jax
import jax.numpy as jnp
from jax import lax

B = 256
P_SIZE = 256
LIVE_DEV = 192
SHARD_SAMPLES = 6144
SAMPLES = 49152
M = 32768
NBIN = 256
N_SAMP = 8
N_VAR = 32


def shard_layout(key):
    spare = B - LIVE_DEV
    base_key = jax.random.fold_in(key, 101)
    key_order, key_amount, key_perm = jax.random.split(base_key, 3)
    bin_order = jax.vmap(lambda one_key: jax.random.permutation(one_key, N_VAR))(jax.random.split(key_order, N_SAMP)).astype(jnp.int32)
    amounts = jax.random.randint(key_amount, (N_SAMP, N_VAR // 2), 0, spare + 1).astype(jnp.int32)
    amounts = amounts.at[:, 0].set(spare)
    signed = jnp.stack([amounts, -amounts], axis=2).reshape(N_SAMP, N_VAR)
    deficit_pos = spare + signed
    shard_rows = jnp.arange(N_SAMP, dtype=jnp.int32)[:, None]
    deficits = jnp.zeros((N_SAMP, N_VAR), jnp.int32).at[shard_rows, bin_order].set(deficit_pos)
    bin_fill = (B - deficits).astype(jnp.int32)
    counter = jnp.arange(SHARD_SAMPLES, dtype=jnp.int32)

    def shard_slots(fill_row, one_key):
        bin_ends = jnp.cumsum(fill_row).astype(jnp.int32)
        bin_index = jnp.sum((counter[:, None] >= bin_ends[None, :]).astype(jnp.int32), axis=1)
        bin_starts = bin_ends - fill_row
        live_slots = bin_index * B + counter - bin_starts[bin_index]
        return live_slots[jax.random.permutation(one_key, SHARD_SAMPLES)].astype(jnp.int32)
    slots = jax.vmap(shard_slots)(bin_fill, jax.random.split(key_perm, N_SAMP)).reshape(SAMPLES)
    return (bin_fill, slots)


def draw_bin_sizes(key, part):
    return shard_layout(key)[0]


def draw_slot_of(key, part):
    return shard_layout(key)[1]


def draw_phenotype(key, part):
    key_a, key_b, key_c = jax.random.split(jax.random.fold_in(key, 7), 3)
    row_total = B * NBIN
    base_draw = jax.random.normal(key_a, (row_total, P_SIZE), jnp.float32)
    base_draw = jnp.clip(base_draw, -5.0, 5.0)
    row_scale = jnp.exp(jax.random.uniform(key_b, (row_total, 1), jnp.float32, 0.0, math.log(10.0)))
    trait_scale = jnp.exp(jax.random.uniform(key_c, (1, P_SIZE), jnp.float32, 0.0, math.log(10.0)))
    rising = 3.0 ** (jnp.arange(row_total, dtype=jnp.float32) / row_total)[:, None]
    return (base_draw * row_scale * trait_scale * rising).astype(jnp.bfloat16)


def draw_inverse_blocks(key, part):
    key_a, key_b = jax.random.split(jax.random.fold_in(key, 11), 2)
    spread = 0.5 / math.sqrt(B)
    raw_draw = jnp.clip(jax.random.normal(key_a, (NBIN, B, B), jnp.float32), -1.73, 1.73) * spread
    symmetric = 0.5 * (raw_draw + jnp.swapaxes(raw_draw, 1, 2))
    identity = jnp.eye(B, dtype=jnp.float32)[None, :, :]
    diagonal = 1.0 + jax.random.uniform(key_b, (NBIN, B, 1), jnp.float32, 0.0, 1.0)
    return symmetric * (1.0 - identity) + diagonal * identity


def block_levels(own_key, extent, shards, smallest, largest):
    def one(dim, blocks):
        draws = jax.random.uniform(jax.random.fold_in(jax.random.fold_in(own_key, 6), dim), (blocks,), jnp.float32, smallest / len(shards), largest / len(shards))
        return jnp.repeat(jnp.exp(draws), extent[dim] // blocks).reshape((-1,) + (1,) * (len(extent) - dim - 1))

    factor_of = one(*shards[0])
    for cut in shards[1:]:
        factor_of = factor_of * one(*cut)
    return factor_of


def setup_inputs(seed: int = 0) -> dict:
    splits = jax.random.split(jax.random.key(seed), 6)
    phenotype = draw_phenotype(jax.random.fold_in(splits[5], 71), 0)
    inverse_blocks = draw_inverse_blocks(jax.random.fold_in(splits[5], 71), 0)
    bin_sizes = draw_bin_sizes(jax.random.fold_in(splits[5], 71), 0)
    slot_of = draw_slot_of(jax.random.fold_in(splits[5], 71), 0)
    dosages = jnp.clip(2.0 * jax.random.uniform(splits[4], (SAMPLES, M), jnp.float32) ** block_levels(splits[4], (SAMPLES, M), ((0, 8), (1, 32)), -0.2, 0.2), 0.0, 2.0).astype(jnp.bfloat16)
    return dict(phenotype=phenotype, inverse_blocks=inverse_blocks, bin_sizes=bin_sizes, slot_of=slot_of, dosages=dosages)


epsilon = 1e-06

def reference(phenotype, inverse_blocks, bin_sizes, slot_of, dosages):
    bin_count = inverse_blocks.shape[0]
    bin_fill = bin_sizes.reshape(bin_count)
    position = jnp.arange(B, dtype=jnp.int32)
    live_mask = (position[None, :] < bin_fill[:, None]).astype(jnp.float32)
    masked_pheno = phenotype.astype(jnp.float32).reshape(bin_count, B, P_SIZE) * live_mask[:, :, None]
    whitened = jnp.einsum('bij,bjp->bip', inverse_blocks, masked_pheno, precision=lax.Precision.HIGHEST) * live_mask[:, :, None]
    trait_scale = lax.optimization_barrier(jnp.sum(masked_pheno * whitened, axis=(0, 1)))
    white_rows = whitened.astype(jnp.bfloat16).reshape(N_SAMP, N_VAR * B, P_SIZE)
    slot_weight = jnp.diagonal(inverse_blocks, axis1=1, axis2=2).astype(jnp.bfloat16).reshape(N_SAMP, N_VAR * B)
    shard_slots = slot_of.reshape(N_SAMP, SHARD_SAMPLES)
    shard_rows = dosages.reshape(N_SAMP, SHARD_SAMPLES, M)
    scores = jnp.zeros((M, P_SIZE), jnp.float32)
    variance = jnp.zeros((M,), jnp.float32)
    for shard in range(N_SAMP):
        picked = jnp.take(white_rows[shard], shard_slots[shard], axis=0)
        scores = scores + lax.dot_general(shard_rows[shard], picked, (((0,), (0,)), ((), ())), preferred_element_type=jnp.float32)
        sample_weight = jnp.take(slot_weight[shard], shard_slots[shard]).astype(jnp.float32)
        squares = shard_rows[shard].astype(jnp.float32) ** 2
        variance = variance + jnp.dot(sample_weight, squares, precision=lax.Precision.HIGHEST)
    return scores / jnp.sqrt(variance[:, None] * trait_scale[None, :] / SAMPLES + epsilon)
```

```python
import heapq

import jax
import jax.numpy as jnp
from jax import lax
from jax.experimental import pallas as pl
from jax.experimental.pallas import tpu as pltpu
from jax.sharding import Mesh
from jax.sharding import PartitionSpec as P

MESH = pl.DeviceIdType.MESH
X, CORE, Z, Y = "samp_0", "samp_1", "var_0", "var_1"
NX, NZ, NY = 4, 8, 4
NBINS = NZ * NY
B = 256
T = 256
N = 6144
M = 1024
N_ALL = 49152
EPS = 1e-6
MSG = T + 16
TS = 128 * 10

PARTS = {"A": (0, 160), "B": (160, MSG - 160)}
HOPS_Z = [0, 1, -1, 2, -2, 3, -3, 4]
HOPS_Y = [0, 1, -1, 2]


def slot(a, b):
    return HOPS_Z.index(a) * NY + HOPS_Y.index(b)


def forwards(part, a, b):
    along_z, along_y = [], []
    if 0 <= a < 4:
        along_z.append((Z, 1, a + 1, b))
    if -3 < a <= 0:
        along_z.append((Z, -1, a - 1, b))
    if 0 <= b < 2:
        along_y.append((Y, 1, a, b + 1))
    if -1 < b <= 0:
        along_y.append((Y, -1, a, b - 1))
    if part == "A":
        return (along_z if b == 0 else []) + along_y
    return along_z + (along_y if a == 0 else [])


def gather_order(rate, latency, single):
    queue = {(ax, d): [] for ax in (Z, Y) for d in (1, -1)}
    arriving, order, step, now, count = [], [], 0.02, 0.0, 0

    def send(p, a, b):
        for ax, d, a2, b2 in forwards(p, a, b):
            queue[(ax, d)].append([PARTS[p][1] * 0.512, p, a2, b2])

    for p in PARTS:
        order.append((0.0, p, 0, 0))
        send(p, 0, 0)
    while arriving or any(queue.values()):
        now += step
        for ax in (Z, Y):
            active = [d for d in (1, -1) if queue[(ax, d)]]
            for d in active:
                left = (rate / 2 if len(active) == 2 else single) * step
                while left > 0 and queue[(ax, d)]:
                    head = queue[(ax, d)][0]
                    used = min(left, head[0])
                    head[0] -= used
                    left -= used
                    if head[0] <= 1e-9:
                        queue[(ax, d)].pop(0)
                        count += 1
                        heapq.heappush(arriving, (now + latency, count, *head[1:]))
        while arriving and arriving[0][0] <= now:
            when, _, p, a, b = heapq.heappop(arriving)
            order.append((when, p, a, b))
            send(p, a, b)
    return order


GATHER = gather_order(90.0, 3.0, 75.0)
LOADS = 12
ROWS = N // LOADS
GROUP = 32
COST = dict(split=0.6, pick=0.055, multiply=0.22)


def prepare_kernel(pheno_ref, inv_ref, size_ref, slot_ref, msg_ref, sample_ref):
    size = size_ref[0, 0]
    row = lax.broadcasted_iota(jnp.int32, (B, T), 0)
    col = lax.broadcasted_iota(jnp.int32, (B, T), 1)
    omega = inv_ref[0]
    masked = jnp.where(row < size, pheno_ref[...].astype(jnp.float32), 0.0)
    masked_16 = masked.astype(jnp.bfloat16)
    rest, total = omega, None
    for _ in range(3):
        piece = rest.astype(jnp.bfloat16)
        rest = rest - piece.astype(jnp.float32)
        term = jnp.dot(piece, masked_16, preferred_element_type=jnp.float32)
        total = term if total is None else total + term
    white = jnp.where(row < size, total, 0.0)
    scale = jnp.sum(masked * white, axis=0, keepdims=True)
    weight = jnp.sum(jnp.where(row == col, omega, 0.0), axis=0, keepdims=True)
    weight = jnp.where(col[:1] < size, weight, 0.0)
    turned = white.T
    for c in range(2):
        for x in range(4):
            trait = (2 * x + c) * 32
            at = c * 128 + x * 32
            msg_ref[at : at + 32, :] = turned[trait : trait + 32, :].astype(jnp.bfloat16)
    s0 = scale.astype(jnp.bfloat16).astype(jnp.float32)
    s1 = (scale - s0).astype(jnp.bfloat16).astype(jnp.float32)
    s2 = scale - s0 - s1
    line = lax.broadcasted_iota(jnp.int32, (16, T), 0)
    extra = jnp.where(line == 0, weight, jnp.where(line == 1, s0, jnp.where(line == 2, s1, jnp.where(line == 3, s2, 0.0))))
    msg_ref[T:MSG, :] = extra.astype(jnp.bfloat16)

    found = jnp.zeros((128, 128), jnp.float32)
    chunk = 1024
    for k in range(N // chunk):
        slots = slot_ref[:, k * chunk : (k + 1) * chunk]
        high, low = slots // 128, slots % 128
        at = lax.broadcasted_iota(jnp.int32, (128, chunk), 0)
        sample = lax.broadcasted_iota(jnp.int32, (128, chunk), 1) + k * chunk
        digit = jnp.where(at < 64, sample // 128, sample % 128).astype(jnp.float32)
        left = jnp.where(at % 64 == high, digit, 0.0).astype(jnp.bfloat16)
        right = jnp.where(at == low, 1.0, 0.0).astype(jnp.bfloat16)
        found += lax.dot_general(left, right, (((1,), (1,)), ((), ())), preferred_element_type=jnp.float32)
    sample_ref[...] = (found[:64] * 128.0 + found[64:]).astype(jnp.int32)


def prepare(phenotype, inverse_blocks, bin_sizes, slot_of):
    vmem = pl.BlockSpec(memory_space=pltpu.VMEM)
    return pl.pallas_call(
        prepare_kernel,
        name="prepare",
        out_shape=(jax.ShapeDtypeStruct((MSG, T), jnp.bfloat16), jax.ShapeDtypeStruct((64, 128), jnp.int32)),
        in_specs=[vmem, vmem, pl.BlockSpec(memory_space=pltpu.SMEM), vmem],
        out_specs=(vmem, vmem),
    )(phenotype, inverse_blocks, bin_sizes, slot_of.reshape(1, N))


def scores_kernel(
    sample_ref, msg_ref, dosage_ref, out_ref,
    split, ordered, got, acc, var_acc,
    half_out, half_in, part_out, part_in, small_out, small_in,
    send_sem, recv_sem, load_sem, own_sem, half_send, half_recv, part_send, part_recv, small_send, small_recv,
):
    x, core, z, y = (lax.axis_index(name) for name in (X, CORE, Z, Y))
    forward = 1 - 2 * core
    neighbour = {
        (Z, 1): (x, core, (z + forward + NZ) % NZ, y),
        (Z, -1): (x, core, (z - forward + NZ) % NZ, y),
        (Y, 1): (x, core, z, (y + forward + NY) % NY),
        (Y, -1): (x, core, z, (y - forward + NY) % NY),
    }
    sibling = (x, 1 - core, z, y)
    peers = {d: ((x + d) % NX, core, z, y) for d in (1, 2, 3)}
    partners = [*neighbour.values(), sibling, *peers.values()]

    loads = [
        pltpu.make_async_copy(
            dosage_ref.at[pl.ds(i * ROWS, ROWS)], ordered.at[pl.ds(i * ROWS, ROWS)], load_sem.at[i]
        )
        for i in range(LOADS)
    ]
    own = pltpu.make_async_copy(msg_ref, got.at[0], own_sem)
    own.start()
    for load in loads:
        load.start()

    barrier = pltpu.get_barrier_semaphore()
    for partner in partners:
        pl.semaphore_signal(barrier, inc=1, device_id=partner, device_id_type=MESH)
    acc[...] = jnp.zeros_like(acc)
    var_acc[...] = jnp.zeros_like(var_acc)
    own.wait()
    pl.semaphore_wait(barrier, len(partners))

    def remote(source, target, send, recv, device):
        return pltpu.make_async_remote_copy(
            src_ref=source, dst_ref=target, send_sem=send, recv_sem=recv, device_id=device, device_id_type=MESH
        )

    def part_of(p, a, b):
        first, count = PARTS[p]
        return got.at[slot(a, b), pl.ds(first, count)]

    part_index = {p: i for i, p in enumerate(PARTS)}
    sends = []

    def await_and_forward(p, a, b):
        if (a, b) != (0, 0):
            here = part_of(p, a, b)
            remote(here, here, send_sem.at[0], recv_sem.at[part_index[p], slot(a, b)], sibling).wait_recv()
        for ax, d, a2, b2 in forwards(p, a, b):
            copy = remote(
                part_of(p, a, b), part_of(p, a2, b2), send_sem.at[len(sends)],
                recv_sem.at[part_index[p], slot(a2, b2)], neighbour[(ax, d)],
            )
            copy.start()
            sends.append(copy)

    flat = split.reshape(N * 8, 128)

    def split_rows(i):
        loads[i].wait()

        @pl.loop(0, ROWS // 16)
        def _(g):
            row = pl.multiple_of(i * ROWS + g * 16, 16)
            value = ordered[pl.ds(row, 16), :].astype(jnp.float32)
            base = pl.multiple_of(row * 8, 128)
            for h in range(2):
                for j in range(8):
                    flat[pl.ds(base + h * 64 + j, 8, stride=8), :] = value[8 * h : 8 * h + 8, 128 * j : 128 * j + 128]

    def pick_rows(first, last):
        @pl.loop(first, last)
        def _(g):
            t = g // (B // GROUP)
            ia, ib = t // NY, t % NY
            a = (1 - 2 * ((ia + 1) % 2)) * ((ia + 1) // 2)
            b = (1 - 2 * ((ib + 1) % 2)) * ((ib + 1) // 2)
            origin = ((z - forward * a + NZ) % NZ) * NY + (y - forward * b + NY) % NY
            start = origin * B + (g % (B // GROUP)) * GROUP
            for q in range(GROUP // 16):
                rows = jnp.stack([split[sample_ref[start + q * 16 + u]] for u in range(16)], 0)
                turned = pltpu.einshape("kjl->jkl", rows).astype(jnp.bfloat16)
                at = pl.multiple_of(g * GROUP + q * 16, 16)
                for j in range(8):
                    ordered[pl.ds(at, 16), 128 * j : 128 * j + 128] = turned[j]

    def multiply(t):
        @pl.loop(0, M // 256)
        def _(n):
            columns = pl.ds(pl.multiple_of(n * 256, 256), 256)
            right = ordered[pl.ds(t * B, B), columns]
            acc[:, columns] += jnp.dot(got[t, :T, :], right, preferred_element_type=jnp.float32)
            var_acc[:, columns] += jnp.dot(got[t, T:, :], right * right, preferred_element_type=jnp.float32)

    clock = 0.0
    to_split = list(range(LOADS))
    picked, groups = 0, NBINS * B // GROUP
    seen, ready = {}, []

    def work(until):
        nonlocal clock, picked
        while clock < until:
            if to_split:
                split_rows(to_split.pop(0))
                clock += COST["split"]
            elif ready and (ready[0] + 1) * (B // GROUP) <= picked:
                multiply(ready.pop(0))
                clock += COST["multiply"]
            elif picked < groups:
                count = min(B // GROUP, groups - picked)
                pick_rows(picked, picked + count)
                picked += count
                clock += COST["pick"] * count
            else:
                return

    for when, p, a, b in GATHER:
        work(when)
        await_and_forward(p, a, b)
        seen[(a, b)] = seen.get((a, b), 0) + 1
        if seen[(a, b)] == len(PARTS):
            ready.append(slot(a, b))
            ready.sort()
    work(float("inf"))
    for copy in sends:
        copy.wait_send()

    scale = got[0, T + 1 : T + 4, :].astype(jnp.float32).sum(axis=0, keepdims=True)
    for t in range(1, NBINS):
        scale += got[t, T + 1 : T + 4, :].astype(jnp.float32).sum(axis=0, keepdims=True)
    small_out[0, :, :M] = var_acc[0:1, :]
    small_out[0, :, M:] = scale
    smalls = [remote(small_out.at[0], small_in.at[0], small_send.at[0], small_recv.at[0], sibling)]
    smalls[0].start()

    halves = {}
    for d in (2, 1, 3, 0):
        rows = pl.ds(pl.multiple_of((1 - core) * 128 + ((x + d) % NX) * 32, 32), 32)
        half_out[d] = acc[rows, :].astype(jnp.bfloat16)
        halves[d] = remote(half_out.at[d], half_in.at[d], half_send.at[d], half_recv.at[d], sibling)
        halves[d].start()

    smalls[0].wait()
    small_out[1] = small_out[0] + small_in[0]
    for d in (1, 2, 3):
        copy = remote(small_out.at[1], small_in.at[d], small_send.at[d], small_recv.at[d], peers[d])
        copy.start()
        smalls.append(copy)

    pieces = []
    for d in (2, 1, 3, 0):
        rows = pl.ds(pl.multiple_of(core * 128 + ((x + d) % NX) * 32, 32), 32)
        halves[d].wait()
        both = acc[rows, :] + half_in[d].astype(jnp.float32)
        if d == 0:
            total = both
        else:
            part_out[d - 1] = both.astype(jnp.bfloat16)
            copy = remote(part_out.at[d - 1], part_in.at[d - 1], part_send.at[d - 1], part_recv.at[d - 1], peers[d])
            copy.start()
            pieces.append(copy)
    for copy in smalls[1:]:
        copy.wait()
    small = small_out[1] + small_in[1] + small_in[2] + small_in[3]
    variance, scale = small[:, :M], small[:, M:]
    trait = (2 * x + core) * 32 + lax.broadcasted_iota(jnp.int32, (32, T), 0)
    lane = lax.broadcasted_iota(jnp.int32, (32, T), 1)
    share = jnp.sum(jnp.where(lane == trait, scale, 0.0), axis=1, keepdims=True)
    root = lax.rsqrt(variance * share / N_ALL + EPS)
    for copy in pieces:
        copy.wait()
    for d in range(3):
        total += part_in[d].astype(jnp.float32)
    out_ref[...] = total * root


def score(samples, message, dosages):
    vmem = pl.BlockSpec(memory_space=pltpu.VMEM)
    anywhere = pl.BlockSpec(memory_space=pl.ANY)
    dma = pltpu.SemaphoreType.DMA
    n_sends = sum(len(forwards(p, a, b)) for _, p, a, b in GATHER)
    return pl.pallas_call(
        scores_kernel,
        name="scores",
        out_shape=jax.ShapeDtypeStruct((32, M), jnp.float32),
        in_specs=[pl.BlockSpec(memory_space=pltpu.SMEM), anywhere, anywhere],
        out_specs=vmem,
        scratch_shapes=[
            pltpu.VMEM((N, 8, 128), jnp.float32),
            pltpu.VMEM((NBINS * B, M), jnp.bfloat16),
            pltpu.VMEM((NBINS, MSG, B), jnp.bfloat16),
            pltpu.VMEM((T, M), jnp.float32),
            pltpu.VMEM((16, M), jnp.float32),
            pltpu.VMEM((4, 32, M), jnp.bfloat16),
            pltpu.VMEM((4, 32, M), jnp.bfloat16),
            pltpu.VMEM((3, 32, M), jnp.bfloat16),
            pltpu.VMEM((3, 32, M), jnp.bfloat16),
            pltpu.VMEM((2, 1, TS), jnp.float32),
            pltpu.VMEM((4, 1, TS), jnp.float32),
            dma((n_sends,)), dma((2, NBINS)), dma((LOADS,)), dma,
            dma((4,)), dma((4,)), dma((3,)), dma((3,)), dma((4,)), dma((4,)),
        ],
        compiler_params=pltpu.CompilerParams(
            collective_id=0, has_side_effects=True, vmem_limit_bytes=58 << 20
        ),
    )(samples, message, dosages)


def local(phenotype, inverse_blocks, bin_sizes, slot_of, dosages):
    message, samples = prepare(phenotype, inverse_blocks, bin_sizes, slot_of)
    return score(samples.reshape(NBINS * B), message, dosages).T


def solution(mesh):
    split = Mesh(mesh.devices.reshape(NX, 2, NZ, NY), (X, CORE, Z, Y))
    samp, var, both = (X, CORE), (Z, Y), (X, CORE, Z, Y)
    in_specs = (P(both, None), P(both, None, None), P(samp, var), P(samp), P(samp, var))
    return jax.shard_map(local, mesh=split, in_specs=in_specs, out_specs=P(var, samp), check_vma=False)
```

```python
import heapq

import jax
import jax.numpy as jnp
from jax import lax
from jax.experimental import pallas as pl
from jax.experimental.pallas import tpu as pltpu
from jax.sharding import Mesh
from jax.sharding import PartitionSpec as P

MESH = pl.DeviceIdType.MESH
X, CORE, Z, Y = "samp_0", "samp_1", "var_0", "var_1"
NX, NZ, NY = 4, 8, 4
NBINS = NZ * NY
B = 256
T = 256
N = 6144
M = 1024
N_ALL = 49152
EPS = 1e-6
MSG = T + 16
TS = 128 * 10

PARTS = {"A": (0, 160), "B": (160, MSG - 160)}
HOPS_Z = [0, 1, -1, 2, -2, 3, -3, 4]
HOPS_Y = [0, 1, -1, 2]


def slot(a, b):
    return HOPS_Z.index(a) * NY + HOPS_Y.index(b)


def forwards(part, a, b):
    along_z, along_y = [], []
    if 0 <= a < 4:
        along_z.append((Z, 1, a + 1, b))
    if -3 < a <= 0:
        along_z.append((Z, -1, a - 1, b))
    if 0 <= b < 2:
        along_y.append((Y, 1, a, b + 1))
    if -1 < b <= 0:
        along_y.append((Y, -1, a, b - 1))
    if part == "A":
        return (along_z if b == 0 else []) + along_y
    return along_z + (along_y if a == 0 else [])


def gather_order(rate, latency, single):
    queue = {(ax, d): [] for ax in (Z, Y) for d in (1, -1)}
    arriving, order, step, now, count = [], [], 0.02, 0.0, 0

    def send(p, a, b):
        for ax, d, a2, b2 in forwards(p, a, b):
            queue[(ax, d)].append([PARTS[p][1] * 0.512, p, a2, b2])

    for p in PARTS:
        order.append((0.0, p, 0, 0))
        send(p, 0, 0)
    while arriving or any(queue.values()):
        now += step
        for ax in (Z, Y):
            active = [d for d in (1, -1) if queue[(ax, d)]]
            for d in active:
                left = (rate / 2 if len(active) == 2 else single) * step
                while left > 0 and queue[(ax, d)]:
                    head = queue[(ax, d)][0]
                    used = min(left, head[0])
                    head[0] -= used
                    left -= used
                    if head[0] <= 1e-9:
                        queue[(ax, d)].pop(0)
                        count += 1
                        heapq.heappush(arriving, (now + latency, count, *head[1:]))
        while arriving and arriving[0][0] <= now:
            when, _, p, a, b = heapq.heappop(arriving)
            order.append((when, p, a, b))
            send(p, a, b)
    return order


GATHER = gather_order(90.0, 4.0, 75.0)
LOADS = 24
ROWS = N // LOADS
GROUP = 64
PACE, LEAD = 0.8, 0.0
LOADED = (1.5, 0.3)
COST = dict(split=0.3, pick=0.3, multiply=0.58, forward=0.05)


def invert_kernel(slot_ref, sample_ref):
    found = jnp.zeros((128, 128), jnp.float32)
    chunk = 1024
    for k in range(N // chunk):
        slots = slot_ref[:, k * chunk : (k + 1) * chunk]
        high, low = slots // 128, slots % 128
        at = lax.broadcasted_iota(jnp.int32, (128, chunk), 0)
        sample = lax.broadcasted_iota(jnp.int32, (128, chunk), 1) + k * chunk
        digit = jnp.where(at < 64, sample // 128, sample % 128).astype(jnp.float32)
        left = jnp.where(at % 64 == high, digit, 0.0).astype(jnp.bfloat16)
        right = jnp.where(at == low, 1.0, 0.0).astype(jnp.bfloat16)
        found += lax.dot_general(left, right, (((1,), (1,)), ((), ())), preferred_element_type=jnp.float32)
    sample_ref[...] = (found[:64] * 128.0 + found[64:]).astype(jnp.int32)


def invert(slot_of):
    vmem = pl.BlockSpec(memory_space=pltpu.VMEM)
    return pl.pallas_call(
        invert_kernel,
        name="invert",
        out_shape=jax.ShapeDtypeStruct((64, 128), jnp.int32),
        in_specs=[vmem],
        out_specs=vmem,
    )(slot_of.reshape(1, N))


def whiten(pheno_ref, omega_ref, size_ref, message_ref):
    size = size_ref[0, 0]
    row = lax.broadcasted_iota(jnp.int32, (B, T), 0)
    col = lax.broadcasted_iota(jnp.int32, (B, T), 1)
    omega = omega_ref[0]
    masked = jnp.where(row < size, pheno_ref[...].astype(jnp.float32), 0.0)
    masked_16 = masked.astype(jnp.bfloat16)
    rest, total = omega, None
    for _ in range(3):
        piece = rest.astype(jnp.bfloat16)
        rest = rest - piece.astype(jnp.float32)
        term = jnp.dot(piece, masked_16, preferred_element_type=jnp.float32)
        total = term if total is None else total + term
    white = jnp.where(row < size, total, 0.0)
    scale = jnp.sum(masked * white, axis=0, keepdims=True)
    weight = jnp.sum(jnp.where(row == col, omega, 0.0), axis=0, keepdims=True)
    weight = jnp.where(col[:1] < size, weight, 0.0)
    turned = white.T
    for c in range(2):
        for x in range(4):
            trait = (2 * x + c) * 32
            at = c * 128 + x * 32
            message_ref[at : at + 32, :] = turned[trait : trait + 32, :].astype(jnp.bfloat16)
    s0 = scale.astype(jnp.bfloat16).astype(jnp.float32)
    s1 = (scale - s0).astype(jnp.bfloat16).astype(jnp.float32)
    s2 = scale - s0 - s1
    line = lax.broadcasted_iota(jnp.int32, (16, T), 0)
    extra = jnp.where(line == 0, weight, jnp.where(line == 1, s0, jnp.where(line == 2, s1, jnp.where(line == 3, s2, 0.0))))
    message_ref[T:MSG, :] = extra.astype(jnp.bfloat16)


def scores_kernel(
    size_ref, sample_hbm, pheno_hbm, omega_hbm, dosage_ref, out_ref,
    sample_ref, pheno_ref, omega_ref, split, ordered, got, acc, var_acc, scale_acc,
    half_out, half_in, part_out, part_in, small_out, small_in,
    send_sem, recv_sem, load_sem, own_sem, half_send, half_recv, part_send, part_recv, small_send, small_recv,
):
    x, core, z, y = (lax.axis_index(name) for name in (X, CORE, Z, Y))
    forward = 1 - 2 * core
    neighbour = {
        (Z, 1): (x, core, (z + forward + NZ) % NZ, y),
        (Z, -1): (x, core, (z - forward + NZ) % NZ, y),
        (Y, 1): (x, core, z, (y + forward + NY) % NY),
        (Y, -1): (x, core, z, (y - forward + NY) % NY),
    }
    sibling = (x, 1 - core, z, y)
    peers = {d: ((x + d) % NX, core, z, y) for d in (1, 2, 3)}
    partners = [*neighbour.values(), sibling, *peers.values()]

    loads = [
        pltpu.make_async_copy(
            dosage_ref.at[pl.ds(i * ROWS, ROWS)], ordered.at[pl.ds(i * ROWS, ROWS)], load_sem.at[i]
        )
        for i in range(LOADS)
    ]
    own = [
        pltpu.make_async_copy(source, target, own_sem.at[i])
        for i, (source, target) in enumerate(
            [(omega_hbm, omega_ref), (pheno_hbm, pheno_ref), (sample_hbm, sample_ref)]
        )
    ]
    for copy in own:
        copy.start()
    barrier = pltpu.get_barrier_semaphore()
    for partner in partners:
        pl.semaphore_signal(barrier, inc=1, device_id=partner, device_id_type=MESH)
    own[0].wait()
    own[1].wait()
    whiten(pheno_ref, omega_ref, size_ref, got.at[0])
    pl.semaphore_wait(barrier, len(partners))

    def remote(source, target, send, recv, device):
        return pltpu.make_async_remote_copy(
            src_ref=source, dst_ref=target, send_sem=send, recv_sem=recv, device_id=device, device_id_type=MESH
        )

    def part_of(p, a, b):
        first, count = PARTS[p]
        return got.at[slot(a, b), pl.ds(first, count)]

    part_index = {p: i for i, p in enumerate(PARTS)}
    sends = []

    def await_and_forward(p, a, b):
        if (a, b) != (0, 0):
            here = part_of(p, a, b)
            remote(here, here, send_sem.at[0], recv_sem.at[part_index[p], slot(a, b)], sibling).wait_recv()
        for ax, d, a2, b2 in forwards(p, a, b):
            copy = remote(
                part_of(p, a, b), part_of(p, a2, b2), send_sem.at[len(sends)],
                recv_sem.at[part_index[p], slot(a2, b2)], neighbour[(ax, d)],
            )
            copy.start()
            sends.append(copy)

    flat = split.reshape(N * 8, 128)

    def split_rows(i):
        loads[i].wait()

        @pl.loop(0, ROWS // 16)
        def _(g):
            row = pl.multiple_of(i * ROWS + g * 16, 16)
            value = ordered[pl.ds(row, 16), :].astype(jnp.float32)
            base = pl.multiple_of(row * 8, 128)
            for h in range(2):
                for j in range(8):
                    flat[pl.ds(base + h * 64 + j, 8, stride=8), :] = value[8 * h : 8 * h + 8, 128 * j : 128 * j + 128]

    def pick_rows(t):
        a, b = HOPS_Z[t // NY], HOPS_Y[t % NY]
        origin = ((z - forward * a + NZ) % NZ) * NY + (y - forward * b + NY) % NY
        first = origin * B

        @pl.loop(0, B // GROUP)
        def _(g):
            start = first + g * GROUP
            for q in range(GROUP // 16):
                rows = jnp.stack([split[sample_ref[start + q * 16 + u]] for u in range(16)], 0)
                turned = pltpu.einshape("kjl->jkl", rows).astype(jnp.bfloat16)
                at = pl.multiple_of(t * B + g * GROUP + q * 16, 16)
                for j in range(8):
                    ordered[pl.ds(at, 16), 128 * j : 128 * j + 128] = turned[j]

    def multiply(s):
        left = jnp.concatenate([got[2 * s, :T, :], got[2 * s + 1, :T, :]], axis=1)
        extra = jnp.concatenate([got[2 * s, T:, :], got[2 * s + 1, T:, :]], axis=1)
        right = ordered[pl.ds(s * 2 * B, 2 * B), :]
        acc[...] += jnp.dot(left, right, preferred_element_type=jnp.float32)
        var_acc[...] += jnp.dot(extra, right * right, preferred_element_type=jnp.float32)
        scale_acc[...] += extra[:, :B].astype(jnp.float32) + extra[:, B:].astype(jnp.float32)

    clock = 0.0
    to_split = list(range(LOADS))
    picked = 0
    seen, ready = {}, []

    def work(until):
        nonlocal clock, picked
        while clock < until:
            if to_split:
                clock = max(clock, LOADED[0] + LOADED[1] * (to_split[0] + 1))
                if clock >= until:
                    return
                split_rows(to_split.pop(0))
                clock += COST["split"]
            elif ready and (ready[0] + 1) * 2 <= picked:
                multiply(ready.pop(0))
                clock += COST["multiply"]
            elif picked < NBINS:
                pick_rows(picked)
                picked += 1
                clock += COST["pick"]
            else:
                return

    for n, (when, p, a, b) in enumerate(GATHER):
        when = max(0.0, when * PACE - LEAD)
        work(when)
        await_and_forward(p, a, b)
        clock = max(clock, when) + COST["forward"]
        pair = slot(a, b) // 2
        seen[pair] = seen.get(pair, 0) + 1
        if seen[pair] == 2 * len(PARTS):
            ready.append(pair)
            ready.sort()
        if n == len(PARTS) - 1:
            for load in loads:
                load.start()
            acc[...] = jnp.zeros_like(acc)
            var_acc[...] = jnp.zeros_like(var_acc)
            scale_acc[...] = jnp.zeros_like(scale_acc)
            own[2].wait()
    work(float("inf"))
    for copy in sends:
        copy.wait_send()

    scale = scale_acc[1:2, :] + scale_acc[2:3, :] + scale_acc[3:4, :]
    small_out[0, :, :M] = var_acc[0:1, :]
    small_out[0, :, M:] = scale
    smalls = [remote(small_out.at[0], small_in.at[0], small_send.at[0], small_recv.at[0], sibling)]
    smalls[0].start()

    halves = {}
    for d in (2, 1, 3, 0):
        rows = pl.ds(pl.multiple_of((1 - core) * 128 + ((x + d) % NX) * 32, 32), 32)
        half_out[d] = acc[rows, :].astype(jnp.bfloat16)
        halves[d] = remote(half_out.at[d], half_in.at[d], half_send.at[d], half_recv.at[d], sibling)
        halves[d].start()

    smalls[0].wait()
    small_out[1] = small_out[0] + small_in[0]
    for d in (1, 2, 3):
        copy = remote(small_out.at[1], small_in.at[d], small_send.at[d], small_recv.at[d], peers[d])
        copy.start()
        smalls.append(copy)

    pieces = []
    for d in (2, 1, 3, 0):
        rows = pl.ds(pl.multiple_of(core * 128 + ((x + d) % NX) * 32, 32), 32)
        halves[d].wait()
        both = acc[rows, :] + half_in[d].astype(jnp.float32)
        if d == 0:
            total = both
        else:
            part_out[d - 1] = both.astype(jnp.bfloat16)
            copy = remote(part_out.at[d - 1], part_in.at[d - 1], part_send.at[d - 1], part_recv.at[d - 1], peers[d])
            copy.start()
            pieces.append(copy)
    for copy in smalls[1:]:
        copy.wait()
    small = small_out[1] + small_in[1] + small_in[2] + small_in[3]
    variance, scale = small[:, :M], small[:, M:]
    trait = (2 * x + core) * 32 + lax.broadcasted_iota(jnp.int32, (32, T), 0)
    lane = lax.broadcasted_iota(jnp.int32, (32, T), 1)
    share = jnp.sum(jnp.where(lane == trait, scale, 0.0), axis=1, keepdims=True)
    root = lax.rsqrt(variance * share / N_ALL + EPS)
    for copy in pieces:
        copy.wait()
    for d in range(3):
        total += part_in[d].astype(jnp.float32)
    out_ref[...] = total * root


def score(samples, sizes, phenotype, blocks, dosages):
    vmem = pl.BlockSpec(memory_space=pltpu.VMEM)
    smem = pl.BlockSpec(memory_space=pltpu.SMEM)
    hbm = pl.BlockSpec(memory_space=pltpu.HBM)
    dma = pltpu.SemaphoreType.DMA
    n_sends = sum(len(forwards(p, a, b)) for _, p, a, b in GATHER)
    return pl.pallas_call(
        scores_kernel,
        name="scores",
        out_shape=jax.ShapeDtypeStruct((32, M), jnp.float32),
        in_specs=[smem, hbm, hbm, hbm, hbm],
        out_specs=vmem,
        scratch_shapes=[
            pltpu.SMEM((NBINS * B,), jnp.int32),
            pltpu.VMEM((B, T), jnp.bfloat16),
            pltpu.VMEM((1, B, B), jnp.float32),
            pltpu.VMEM((N, 8, 128), jnp.float32),
            pltpu.VMEM((NBINS * B, M), jnp.bfloat16),
            pltpu.VMEM((NBINS, MSG, B), jnp.bfloat16),
            pltpu.VMEM((T, M), jnp.float32),
            pltpu.VMEM((16, M), jnp.float32),
            pltpu.VMEM((16, T), jnp.float32),
            pltpu.VMEM((4, 32, M), jnp.bfloat16),
            pltpu.VMEM((4, 32, M), jnp.bfloat16),
            pltpu.VMEM((3, 32, M), jnp.bfloat16),
            pltpu.VMEM((3, 32, M), jnp.bfloat16),
            pltpu.VMEM((2, 1, TS), jnp.float32),
            pltpu.VMEM((4, 1, TS), jnp.float32),
            dma((n_sends,)), dma((2, NBINS)), dma((LOADS,)), dma((3,)),
            dma((4,)), dma((4,)), dma((3,)), dma((3,)), dma((4,)), dma((4,)),
        ],
        compiler_params=pltpu.CompilerParams(
            collective_id=0, has_side_effects=True, vmem_limit_bytes=58 << 20
        ),
    )(sizes, samples, phenotype, blocks, dosages)


def local(phenotype, inverse_blocks, bin_sizes, slot_of, dosages):
    samples = invert(slot_of).reshape(NBINS * B)
    return score(samples, bin_sizes, phenotype, inverse_blocks, dosages).T


def solution(mesh):
    split = Mesh(mesh.devices.reshape(NX, 2, NZ, NY), (X, CORE, Z, Y))
    samp, var, both = (X, CORE), (Z, Y), (X, CORE, Z, Y)
    in_specs = (P(both, None), P(both, None, None), P(samp, var), P(samp), P(samp, var))
    return jax.shard_map(local, mesh=split, in_specs=in_specs, out_specs=P(var, samp), check_vma=False)
```

```python
import heapq

import jax
import jax.numpy as jnp
from jax import lax
from jax.experimental import pallas as pl
from jax.experimental.pallas import tpu as pltpu
from jax.sharding import Mesh
from jax.sharding import PartitionSpec as P

MESH = pl.DeviceIdType.MESH
X, CORE, Z, Y = "samp_0", "samp_1", "var_0", "var_1"
NX, NZ, NY = 4, 8, 4
NBINS = NZ * NY
B = 256
T = 256
N = 6144
M = 1024
N_ALL = 49152
EPS = 1e-6
MSG = T + 16
TS = 128 * 10

PARTS = {"A": (0, 160), "B": (160, MSG - 160)}
HOPS_Z = [0, 1, -1, 2, -2, 3, -3, 4]
HOPS_Y = [0, 1, -1, 2]


def slot(a, b):
    return HOPS_Z.index(a) * NY + HOPS_Y.index(b)


def forwards(part, a, b):
    along_z, along_y = [], []
    if 0 <= a < 4:
        along_z.append((Z, 1, a + 1, b))
    if -3 < a <= 0:
        along_z.append((Z, -1, a - 1, b))
    if 0 <= b < 2:
        along_y.append((Y, 1, a, b + 1))
    if -1 < b <= 0:
        along_y.append((Y, -1, a, b - 1))
    if part == "A":
        return (along_z if b == 0 else []) + along_y
    return along_z + (along_y if a == 0 else [])


def gather_order(rate, latency, single):
    queue = {(ax, d): [] for ax in (Z, Y) for d in (1, -1)}
    arriving, order, step, now, count = [], [], 0.02, 0.0, 0

    def send(p, a, b):
        for ax, d, a2, b2 in forwards(p, a, b):
            queue[(ax, d)].append([PARTS[p][1] * 0.512, p, a2, b2])

    for p in PARTS:
        order.append((0.0, p, 0, 0))
        send(p, 0, 0)
    while arriving or any(queue.values()):
        now += step
        for ax in (Z, Y):
            active = [d for d in (1, -1) if queue[(ax, d)]]
            for d in active:
                left = (rate / 2 if len(active) == 2 else single) * step
                while left > 0 and queue[(ax, d)]:
                    head = queue[(ax, d)][0]
                    used = min(left, head[0])
                    head[0] -= used
                    left -= used
                    if head[0] <= 1e-9:
                        queue[(ax, d)].pop(0)
                        count += 1
                        heapq.heappush(arriving, (now + latency, count, *head[1:]))
        while arriving and arriving[0][0] <= now:
            when, _, p, a, b = heapq.heappop(arriving)
            order.append((when, p, a, b))
            send(p, a, b)
    return order


GATHER = gather_order(90.0, 4.0, 75.0)
LOADS = 24
ROWS = N // LOADS
GROUP = 64
PACE, LEAD = 0.87, 0.0
LOADED = (1.5, 0.3)
COST = dict(split=0.3, pick=0.3, multiply=0.58, forward=0.05)


def invert_kernel(slot_ref, sample_ref):
    found = jnp.zeros((128, 128), jnp.float32)
    chunk = 1024
    for k in range(N // chunk):
        slots = slot_ref[:, k * chunk : (k + 1) * chunk]
        high, low = slots >> 7, slots & 127
        at = lax.broadcasted_iota(jnp.int32, (128, chunk), 0)
        sample = lax.broadcasted_iota(jnp.int32, (128, chunk), 1) + k * chunk
        digit = jnp.where(at < 64, sample >> 7, sample & 127).astype(jnp.float32)
        left = jnp.where((at & 63) == high, digit, 0.0).astype(jnp.bfloat16)
        right = jnp.where(at == low, 1.0, 0.0).astype(jnp.bfloat16)
        found += lax.dot_general(left, right, (((1,), (1,)), ((), ())), preferred_element_type=jnp.float32)
    sample_ref[...] = (found[:64] * 128.0 + found[64:]).astype(jnp.int32)


def invert(slot_of):
    vmem = pl.BlockSpec(memory_space=pltpu.VMEM)
    return pl.pallas_call(
        invert_kernel,
        name="invert",
        cost_estimate=pl.CostEstimate(flops=4_000_000_000, bytes_accessed=60_000, transcendentals=0),
        out_shape=jax.ShapeDtypeStruct((64, 128), jnp.int32),
        in_specs=[vmem],
        out_specs=vmem,
    )(slot_of.reshape(1, N))


def whiten(pheno_ref, omega_ref, size_ref, message_ref):
    size = size_ref[0, 0]
    row = lax.broadcasted_iota(jnp.int32, (B, T), 0)
    col = lax.broadcasted_iota(jnp.int32, (B, T), 1)
    omega = omega_ref[0]
    masked = jnp.where(row < size, pheno_ref[...].astype(jnp.float32), 0.0)
    masked_16 = masked.astype(jnp.bfloat16)
    rest, total = omega, None
    for _ in range(3):
        piece = rest.astype(jnp.bfloat16)
        rest = rest - piece.astype(jnp.float32)
        term = jnp.dot(piece, masked_16, preferred_element_type=jnp.float32)
        total = term if total is None else total + term
    white = jnp.where(row < size, total, 0.0)
    scale = jnp.sum(masked * white, axis=0, keepdims=True)
    weight = jnp.sum(jnp.where(row == col, omega, 0.0), axis=0, keepdims=True)
    weight = jnp.where(col[:1] < size, weight, 0.0)
    turned = white.T
    for c in range(2):
        for x in range(4):
            trait = (2 * x + c) * 32
            at = c * 128 + x * 32
            message_ref[at : at + 32, :] = turned[trait : trait + 32, :].astype(jnp.bfloat16)
    s0 = scale.astype(jnp.bfloat16).astype(jnp.float32)
    s1 = (scale - s0).astype(jnp.bfloat16).astype(jnp.float32)
    s2 = scale - s0 - s1
    line = lax.broadcasted_iota(jnp.int32, (16, T), 0)
    extra = jnp.where(line == 0, weight, jnp.where(line == 1, s0, jnp.where(line == 2, s1, jnp.where(line == 3, s2, 0.0))))
    message_ref[T:MSG, :] = extra.astype(jnp.bfloat16)


def scores_kernel(
    size_ref, sample_hbm, pheno_hbm, omega_hbm, dosage_ref, out_ref,
    sample_ref, pheno_ref, omega_ref, split, ordered, got, acc, var_acc, scale_acc,
    half_out, half_in, part_out, part_in, small_out, small_in,
    send_sem, recv_sem, load_sem, own_sem, half_send, half_recv, part_send, part_recv, small_send, small_recv,
):
    x, core, z, y = (lax.axis_index(name) for name in (X, CORE, Z, Y))
    forward = 1 - 2 * core
    neighbour = {
        (Z, 1): (x, core, (z + forward + NZ) % NZ, y),
        (Z, -1): (x, core, (z - forward + NZ) % NZ, y),
        (Y, 1): (x, core, z, (y + forward + NY) % NY),
        (Y, -1): (x, core, z, (y - forward + NY) % NY),
    }
    sibling = (x, 1 - core, z, y)
    peers = {d: ((x + d) % NX, core, z, y) for d in (1, 2, 3)}
    partners = [*neighbour.values(), sibling, *peers.values()]

    loads = [
        pltpu.make_async_copy(
            dosage_ref.at[pl.ds(i * ROWS, ROWS)], ordered.at[pl.ds(i * ROWS, ROWS)], load_sem.at[i]
        )
        for i in range(LOADS)
    ]
    own = [
        pltpu.make_async_copy(source, target, own_sem.at[i])
        for i, (source, target) in enumerate(
            [(omega_hbm, omega_ref), (pheno_hbm, pheno_ref), (sample_hbm, sample_ref)]
        )
    ]
    for copy in own:
        copy.start()
    barrier = pltpu.get_barrier_semaphore()
    for partner in partners:
        pl.semaphore_signal(barrier, inc=1, device_id=partner, device_id_type=MESH)
    own[0].wait()
    own[1].wait()
    whiten(pheno_ref, omega_ref, size_ref, got.at[0])
    pl.semaphore_wait(barrier, len(partners))

    def remote(source, target, send, recv, device):
        return pltpu.make_async_remote_copy(
            src_ref=source, dst_ref=target, send_sem=send, recv_sem=recv, device_id=device, device_id_type=MESH
        )

    def part_of(p, a, b):
        first, count = PARTS[p]
        return got.at[slot(a, b), pl.ds(first, count)]

    part_index = {p: i for i, p in enumerate(PARTS)}
    sends = []

    def await_and_forward(p, a, b):
        if (a, b) != (0, 0):
            here = part_of(p, a, b)
            remote(here, here, send_sem.at[0], recv_sem.at[part_index[p], slot(a, b)], sibling).wait_recv()
        for ax, d, a2, b2 in forwards(p, a, b):
            copy = remote(
                part_of(p, a, b), part_of(p, a2, b2), send_sem.at[len(sends)],
                recv_sem.at[part_index[p], slot(a2, b2)], neighbour[(ax, d)],
            )
            copy.start()
            sends.append(copy)

    flat = split.reshape(N * 8, 128)

    def split_rows(i):
        loads[i].wait()

        @pl.loop(0, ROWS // 16)
        def _(g):
            row = pl.multiple_of(i * ROWS + g * 16, 16)
            value = ordered[pl.ds(row, 16), :].astype(jnp.float32)
            base = pl.multiple_of(row * 8, 128)
            for h in range(2):
                for j in range(8):
                    flat[pl.ds(base + h * 64 + j, 8, stride=8), :] = value[8 * h : 8 * h + 8, 128 * j : 128 * j + 128]

    def pick_rows(t):
        a, b = HOPS_Z[t // NY], HOPS_Y[t % NY]
        origin = ((z - forward * a + NZ) % NZ) * NY + (y - forward * b + NY) % NY
        first = origin * B

        @pl.loop(0, B // GROUP)
        def _(g):
            start = first + g * GROUP
            for q in range(GROUP // 16):
                rows = jnp.stack([split[sample_ref[start + q * 16 + u]] for u in range(16)], 0)
                turned = pltpu.einshape("kjl->jkl", rows).astype(jnp.bfloat16)
                at = pl.multiple_of(t * B + g * GROUP + q * 16, 16)
                for j in range(8):
                    ordered[pl.ds(at, 16), 128 * j : 128 * j + 128] = turned[j]

    def multiply(s):
        left = jnp.concatenate([got[2 * s, :T, :], got[2 * s + 1, :T, :]], axis=1)
        extra = jnp.concatenate([got[2 * s, T:, :], got[2 * s + 1, T:, :]], axis=1)
        right = ordered[pl.ds(s * 2 * B, 2 * B), :]
        acc[...] += jnp.dot(left, right, preferred_element_type=jnp.float32)
        var_acc[...] += jnp.dot(extra, right * right, preferred_element_type=jnp.float32)
        scale_acc[...] += extra[:, :B].astype(jnp.float32) + extra[:, B:].astype(jnp.float32)

    clock = 0.0
    to_split = list(range(LOADS))
    picked = 0
    seen, ready = {}, []

    def work(until):
        nonlocal clock, picked
        while clock < until:
            if to_split:
                clock = max(clock, LOADED[0] + LOADED[1] * (to_split[0] + 1))
                if clock >= until:
                    return
                split_rows(to_split.pop(0))
                clock += COST["split"]
            elif ready and (ready[0] + 1) * 2 <= picked:
                multiply(ready.pop(0))
                clock += COST["multiply"]
            elif picked < NBINS:
                pick_rows(picked)
                picked += 1
                clock += COST["pick"]
            else:
                return

    for n, (when, p, a, b) in enumerate(GATHER):
        when = max(0.0, when * PACE - LEAD)
        work(when)
        await_and_forward(p, a, b)
        clock = max(clock, when) + COST["forward"]
        pair = slot(a, b) // 2
        seen[pair] = seen.get(pair, 0) + 1
        if seen[pair] == 2 * len(PARTS):
            ready.append(pair)
            ready.sort()
        if n == len(PARTS) - 1:
            for load in loads:
                load.start()
            acc[...] = jnp.zeros_like(acc)
            var_acc[...] = jnp.zeros_like(var_acc)
            scale_acc[...] = jnp.zeros_like(scale_acc)
            own[2].wait()
    work(float("inf"))
    scale = scale_acc[1:2, :] + scale_acc[2:3, :] + scale_acc[3:4, :]
    small_out[0, :, :M] = var_acc[0:1, :]
    small_out[0, :, M:] = scale
    smalls = [remote(small_out.at[0], small_in.at[0], small_send.at[0], small_recv.at[0], sibling)]
    smalls[0].start()

    halves = {}
    for d in (2, 1, 3, 0):
        rows = pl.ds(pl.multiple_of((1 - core) * 128 + ((x + d) % NX) * 32, 32), 32)
        half_out[d] = acc[rows, :].astype(jnp.bfloat16)
        halves[d] = remote(half_out.at[d], half_in.at[d], half_send.at[d], half_recv.at[d], sibling)
        halves[d].start()

    pieces = []
    for d in (2, 1, 3, 0):
        rows = pl.ds(pl.multiple_of(core * 128 + ((x + d) % NX) * 32, 32), 32)
        halves[d].wait()
        both = acc[rows, :] + half_in[d].astype(jnp.float32)
        if d == 0:
            total = both
        else:
            part_out[d - 1] = both.astype(jnp.bfloat16)
            copy = remote(part_out.at[d - 1], part_in.at[d - 1], part_send.at[d - 1], part_recv.at[d - 1], peers[d])
            copy.start()
            pieces.append(copy)
        if d == 2:
            smalls[0].wait()
            small_out[1] = small_out[0] + small_in[0]
            for far in (2, 1, 3):
                copy = remote(small_out.at[1], small_in.at[far], small_send.at[far], small_recv.at[far], peers[far])
                copy.start()
                smalls.append(copy)
    for copy in sends:
        copy.wait_send()
    for copy in smalls[1:]:
        copy.wait()
    small = small_out[1] + small_in[1] + small_in[2] + small_in[3]
    variance, scale = small[:, :M], small[:, M:]
    trait = (2 * x + core) * 32 + lax.broadcasted_iota(jnp.int32, (32, T), 0)
    lane = lax.broadcasted_iota(jnp.int32, (32, T), 1)
    share = jnp.sum(jnp.where(lane == trait, scale, 0.0), axis=1, keepdims=True)
    root = lax.rsqrt(variance * share / N_ALL + EPS)
    for copy in pieces:
        copy.wait()
    for d in range(3):
        total += part_in[d].astype(jnp.float32)
    out_ref[...] = total * root


def score(samples, sizes, phenotype, blocks, dosages):
    vmem = pl.BlockSpec(memory_space=pltpu.VMEM)
    smem = pl.BlockSpec(memory_space=pltpu.SMEM)
    hbm = pl.BlockSpec(memory_space=pltpu.HBM)
    dma = pltpu.SemaphoreType.DMA
    n_sends = sum(len(forwards(p, a, b)) for _, p, a, b in GATHER)
    return pl.pallas_call(
        scores_kernel,
        name="scores",
        out_shape=jax.ShapeDtypeStruct((32, M), jnp.float32),
        in_specs=[smem, hbm, hbm, hbm, hbm],
        out_specs=vmem,
        scratch_shapes=[
            pltpu.SMEM((NBINS * B,), jnp.int32),
            pltpu.VMEM((B, T), jnp.bfloat16),
            pltpu.VMEM((1, B, B), jnp.float32),
            pltpu.VMEM((N, 8, 128), jnp.float32),
            pltpu.VMEM((NBINS * B, M), jnp.bfloat16),
            pltpu.VMEM((NBINS, MSG, B), jnp.bfloat16),
            pltpu.VMEM((T, M), jnp.float32),
            pltpu.VMEM((16, M), jnp.float32),
            pltpu.VMEM((16, T), jnp.float32),
            pltpu.VMEM((4, 32, M), jnp.bfloat16),
            pltpu.VMEM((4, 32, M), jnp.bfloat16),
            pltpu.VMEM((3, 32, M), jnp.bfloat16),
            pltpu.VMEM((3, 32, M), jnp.bfloat16),
            pltpu.VMEM((2, 1, TS), jnp.float32),
            pltpu.VMEM((4, 1, TS), jnp.float32),
            dma((n_sends,)), dma((2, NBINS)), dma((LOADS,)), dma((3,)),
            dma((4,)), dma((4,)), dma((3,)), dma((3,)), dma((4,)), dma((4,)),
        ],
        compiler_params=pltpu.CompilerParams(
            collective_id=0, has_side_effects=True, vmem_limit_bytes=52 << 20
        ),
    )(sizes, samples, phenotype, blocks, dosages)


def local(phenotype, inverse_blocks, bin_sizes, slot_of, dosages):
    samples = invert(slot_of).reshape(NBINS * B)
    return score(samples, bin_sizes, phenotype, inverse_blocks, dosages).T


def solution(mesh):
    split = Mesh(mesh.devices.reshape(NX, 2, NZ, NY), (X, CORE, Z, Y))
    samp, var, both = (X, CORE), (Z, Y), (X, CORE, Z, Y)
    in_specs = (P(both, None), P(both, None, None), P(samp, var), P(samp), P(samp, var))
    return jax.shard_map(local, mesh=split, in_specs=in_specs, out_specs=P(var, samp), check_vma=False)
```

```python
import heapq

import jax
import jax.numpy as jnp
from jax import lax
from jax.experimental import pallas as pl
from jax.experimental.pallas import tpu as pltpu
from jax.sharding import Mesh
from jax.sharding import PartitionSpec as P

MESH = pl.DeviceIdType.MESH
X, CORE, Z, Y = "samp_0", "samp_1", "var_0", "var_1"
NX, NZ, NY = 4, 8, 4
NBINS = NZ * NY
B = 256
T = 256
N = 6144
M = 1024
N_ALL = 49152
EPS = 1e-6
MSG = T + 16
TS = 128 * 10

PARTS = {"A": (0, 160), "B": (160, MSG - 160)}
HOPS_Z = [0, 1, -1, 2, -2, 3, -3, 4]
HOPS_Y = [0, 1, -1, 2]


def slot(a, b):
    return HOPS_Z.index(a) * NY + HOPS_Y.index(b)


def forwards(part, a, b):
    along_z, along_y = [], []
    if 0 <= a < 4:
        along_z.append((Z, 1, a + 1, b))
    if -3 < a <= 0:
        along_z.append((Z, -1, a - 1, b))
    if 0 <= b < 2:
        along_y.append((Y, 1, a, b + 1))
    if -1 < b <= 0:
        along_y.append((Y, -1, a, b - 1))
    if part == "A":
        return (along_z if b == 0 else []) + along_y
    return along_z + (along_y if a == 0 else [])


def gather_order(rate, latency, single):
    queue = {(ax, d): [] for ax in (Z, Y) for d in (1, -1)}
    arriving, order, step, now, count = [], [], 0.02, 0.0, 0

    def send(p, a, b):
        for ax, d, a2, b2 in forwards(p, a, b):
            queue[(ax, d)].append([PARTS[p][1] * 0.512, p, a2, b2])

    for p in PARTS:
        order.append((0.0, p, 0, 0))
        send(p, 0, 0)
    while arriving or any(queue.values()):
        now += step
        for ax in (Z, Y):
            active = [d for d in (1, -1) if queue[(ax, d)]]
            for d in active:
                left = (rate / 2 if len(active) == 2 else single) * step
                while left > 0 and queue[(ax, d)]:
                    head = queue[(ax, d)][0]
                    used = min(left, head[0])
                    head[0] -= used
                    left -= used
                    if head[0] <= 1e-9:
                        queue[(ax, d)].pop(0)
                        count += 1
                        heapq.heappush(arriving, (now + latency, count, *head[1:]))
        while arriving and arriving[0][0] <= now:
            when, _, p, a, b = heapq.heappop(arriving)
            order.append((when, p, a, b))
            send(p, a, b)
    return order


GATHER = gather_order(90.0, 4.0, 75.0)
LOADS = 24
ROWS = N // LOADS
GROUP = 128
PACE, LEAD = 0.87, 0.0
LOADED = (1.5, 0.3)
COST = dict(split=0.3, pick=0.3, multiply=0.58, forward=0.05)


def invert_kernel(slot_ref, sample_ref):
    found = jnp.zeros((128, 128), jnp.float32)
    chunk = 1024
    for k in range(N // chunk):
        slots = slot_ref[:, k * chunk : (k + 1) * chunk]
        high, low = slots >> 7, slots & 127
        at = lax.broadcasted_iota(jnp.int32, (128, chunk), 0)
        sample = lax.broadcasted_iota(jnp.int32, (128, chunk), 1) + k * chunk
        digit = jnp.where(at < 64, sample >> 7, sample & 127).astype(jnp.float32)
        left = jnp.where((at & 63) == high, digit, 0.0).astype(jnp.bfloat16)
        right = jnp.where(at == low, 1.0, 0.0).astype(jnp.bfloat16)
        found += lax.dot_general(left, right, (((1,), (1,)), ((), ())), preferred_element_type=jnp.float32)
    sample_ref[...] = (found[:64] * 128.0 + found[64:]).astype(jnp.int32)


def invert(slot_of):
    vmem = pl.BlockSpec(memory_space=pltpu.VMEM)
    return pl.pallas_call(
        invert_kernel,
        name="invert",
        cost_estimate=pl.CostEstimate(flops=4_000_000_000, bytes_accessed=60_000, transcendentals=0),
        out_shape=jax.ShapeDtypeStruct((64, 128), jnp.int32),
        in_specs=[vmem],
        out_specs=vmem,
    )(slot_of.reshape(1, N))


def whiten(pheno_ref, omega_ref, size_ref, message_ref):
    size = size_ref[0, 0]
    row = lax.broadcasted_iota(jnp.int32, (B, T), 0)
    col = lax.broadcasted_iota(jnp.int32, (B, T), 1)
    omega = omega_ref[0]
    masked = jnp.where(row < size, pheno_ref[...].astype(jnp.float32), 0.0)
    masked_16 = masked.astype(jnp.bfloat16)
    rest, total = omega, None
    for _ in range(3):
        piece = rest.astype(jnp.bfloat16)
        rest = rest - piece.astype(jnp.float32)
        term = jnp.dot(piece, masked_16, preferred_element_type=jnp.float32)
        total = term if total is None else total + term
    white = jnp.where(row < size, total, 0.0)
    scale = jnp.sum(masked * white, axis=0, keepdims=True)
    weight = jnp.sum(jnp.where(row == col, omega, 0.0), axis=0, keepdims=True)
    weight = jnp.where(col[:1] < size, weight, 0.0)
    turned = white.T
    for c in range(2):
        for x in range(4):
            trait = (2 * x + c) * 32
            at = c * 128 + x * 32
            message_ref[at : at + 32, :] = turned[trait : trait + 32, :].astype(jnp.bfloat16)
    s0 = scale.astype(jnp.bfloat16).astype(jnp.float32)
    s1 = (scale - s0).astype(jnp.bfloat16).astype(jnp.float32)
    s2 = scale - s0 - s1
    line = lax.broadcasted_iota(jnp.int32, (16, T), 0)
    extra = jnp.where(line == 0, weight, jnp.where(line == 1, s0, jnp.where(line == 2, s1, jnp.where(line == 3, s2, 0.0))))
    message_ref[T:MSG, :] = extra.astype(jnp.bfloat16)


def scores_kernel(
    size_ref, sample_hbm, pheno_hbm, omega_hbm, dosage_ref, out_ref,
    sample_ref, pheno_ref, omega_ref, split, ordered, got, acc, var_acc, scale_acc,
    half_out, half_in, part_out, part_in, small_out, small_in,
    send_sem, recv_sem, load_sem, own_sem, half_send, half_recv, part_send, part_recv, small_send, small_recv,
):
    x, core, z, y = (lax.axis_index(name) for name in (X, CORE, Z, Y))
    forward = 1 - 2 * core
    neighbour = {
        (Z, 1): (x, core, (z + forward + NZ) % NZ, y),
        (Z, -1): (x, core, (z - forward + NZ) % NZ, y),
        (Y, 1): (x, core, z, (y + forward + NY) % NY),
        (Y, -1): (x, core, z, (y - forward + NY) % NY),
    }
    sibling = (x, 1 - core, z, y)
    peers = {d: ((x + d) % NX, core, z, y) for d in (1, 2, 3)}
    partners = [*neighbour.values(), sibling, *peers.values()]

    loads = [
        pltpu.make_async_copy(
            dosage_ref.at[pl.ds(i * ROWS, ROWS)], ordered.at[pl.ds(i * ROWS, ROWS)], load_sem.at[i]
        )
        for i in range(LOADS)
    ]
    own = [
        pltpu.make_async_copy(source, target, own_sem.at[i])
        for i, (source, target) in enumerate(
            [(omega_hbm, omega_ref), (pheno_hbm, pheno_ref), (sample_hbm, sample_ref)]
        )
    ]
    for copy in own:
        copy.start()
    barrier = pltpu.get_barrier_semaphore()
    for partner in partners:
        pl.semaphore_signal(barrier, inc=1, device_id=partner, device_id_type=MESH)
    own[0].wait()
    own[1].wait()
    whiten(pheno_ref, omega_ref, size_ref, got.at[0])
    pl.semaphore_wait(barrier, len(partners))

    def remote(source, target, send, recv, device):
        return pltpu.make_async_remote_copy(
            src_ref=source, dst_ref=target, send_sem=send, recv_sem=recv, device_id=device, device_id_type=MESH
        )

    def part_of(p, a, b):
        first, count = PARTS[p]
        return got.at[slot(a, b), pl.ds(first, count)]

    part_index = {p: i for i, p in enumerate(PARTS)}
    sends = []

    def await_and_forward(p, a, b):
        if (a, b) != (0, 0):
            here = part_of(p, a, b)
            remote(here, here, send_sem.at[0], recv_sem.at[part_index[p], slot(a, b)], sibling).wait_recv()
        for ax, d, a2, b2 in forwards(p, a, b):
            copy = remote(
                part_of(p, a, b), part_of(p, a2, b2), send_sem.at[len(sends)],
                recv_sem.at[part_index[p], slot(a2, b2)], neighbour[(ax, d)],
            )
            copy.start()
            sends.append(copy)

    flat = split.reshape(N * 8, 128)

    def split_rows(i):
        loads[i].wait()

        @pl.loop(0, ROWS // 16)
        def _(g):
            row = pl.multiple_of(i * ROWS + g * 16, 16)
            value = ordered[pl.ds(row, 16), :].astype(jnp.float32)
            base = pl.multiple_of(row * 8, 128)
            for h in range(2):
                for j in range(8):
                    flat[pl.ds(base + h * 64 + j, 8, stride=8), :] = value[8 * h : 8 * h + 8, 128 * j : 128 * j + 128]

    def pick_rows(t):
        a, b = HOPS_Z[t // NY], HOPS_Y[t % NY]
        origin = ((z - forward * a + NZ) % NZ) * NY + (y - forward * b + NY) % NY
        first = origin * B

        @pl.loop(0, B // GROUP)
        def _(g):
            start = first + g * GROUP
            for q in range(GROUP // 16):
                rows = jnp.stack([split[sample_ref[start + q * 16 + u]] for u in range(16)], 0)
                turned = pltpu.einshape("kjl->jkl", rows).astype(jnp.bfloat16)
                at = pl.multiple_of(t * B + g * GROUP + q * 16, 16)
                for j in range(8):
                    ordered[pl.ds(at, 16), 128 * j : 128 * j + 128] = turned[j]

    def multiply(s):
        left = jnp.concatenate([got[2 * s, :T, :], got[2 * s + 1, :T, :]], axis=1)
        extra = jnp.concatenate([got[2 * s, T:, :], got[2 * s + 1, T:, :]], axis=1)
        right = ordered[pl.ds(s * 2 * B, 2 * B), :]
        acc[...] += jnp.dot(left, right, preferred_element_type=jnp.float32)
        var_acc[...] += jnp.dot(extra, right * right, preferred_element_type=jnp.float32)
        scale_acc[...] += extra[:, :B].astype(jnp.float32) + extra[:, B:].astype(jnp.float32)

    clock = 0.0
    to_split = list(range(LOADS))
    picked = 0
    seen, ready = {}, []

    def work(until):
        nonlocal clock, picked
        while clock < until:
            if to_split:
                clock = max(clock, LOADED[0] + LOADED[1] * (to_split[0] + 1))
                if clock >= until:
                    return
                split_rows(to_split.pop(0))
                clock += COST["split"]
            elif ready and (ready[0] + 1) * 2 <= picked:
                multiply(ready.pop(0))
                clock += COST["multiply"]
            elif picked < NBINS:
                pick_rows(picked)
                picked += 1
                clock += COST["pick"]
            else:
                return

    for n, (when, p, a, b) in enumerate(GATHER):
        when = max(0.0, when * PACE - LEAD)
        work(when)
        await_and_forward(p, a, b)
        clock = max(clock, when) + COST["forward"]
        pair = slot(a, b) // 2
        seen[pair] = seen.get(pair, 0) + 1
        if seen[pair] == 2 * len(PARTS):
            ready.append(pair)
            ready.sort()
        if n == len(PARTS) - 1:
            for load in loads:
                load.start()
            acc[...] = jnp.zeros_like(acc)
            var_acc[...] = jnp.zeros_like(var_acc)
            scale_acc[...] = jnp.zeros_like(scale_acc)
            own[2].wait()
    work(float("inf"))
    scale = scale_acc[1:2, :] + scale_acc[2:3, :] + scale_acc[3:4, :]
    small_out[0, :, :M] = var_acc[0:1, :]
    small_out[0, :, M:] = scale
    smalls = [remote(small_out.at[0], small_in.at[0], small_send.at[0], small_recv.at[0], sibling)]
    smalls[0].start()

    halves = {}
    for d in (2, 1, 3, 0):
        rows = pl.ds(pl.multiple_of((1 - core) * 128 + ((x + d) % NX) * 32, 32), 32)
        half_out[d] = acc[rows, :].astype(jnp.bfloat16)
        halves[d] = remote(half_out.at[d], half_in.at[d], half_send.at[d], half_recv.at[d], sibling)
        halves[d].start()

    pieces = []
    for d in (2, 1, 3, 0):
        rows = pl.ds(pl.multiple_of(core * 128 + ((x + d) % NX) * 32, 32), 32)
        halves[d].wait()
        both = acc[rows, :] + half_in[d].astype(jnp.float32)
        if d == 0:
            total = both
        else:
            part_out[d - 1] = both.astype(jnp.bfloat16)
            copy = remote(part_out.at[d - 1], part_in.at[d - 1], part_send.at[d - 1], part_recv.at[d - 1], peers[d])
            copy.start()
            pieces.append(copy)
        if d == 2:
            smalls[0].wait()
            small_out[1] = small_out[0] + small_in[0]
            for far in (2, 1, 3):
                copy = remote(small_out.at[1], small_in.at[far], small_send.at[far], small_recv.at[far], peers[far])
                copy.start()
                smalls.append(copy)
    for copy in sends:
        copy.wait_send()
    for copy in smalls[1:]:
        copy.wait()
    small = small_out[1] + small_in[1] + small_in[2] + small_in[3]
    variance, scale = small[:, :M], small[:, M:]
    trait = (2 * x + core) * 32 + lax.broadcasted_iota(jnp.int32, (32, T), 0)
    lane = lax.broadcasted_iota(jnp.int32, (32, T), 1)
    share = jnp.sum(jnp.where(lane == trait, scale, 0.0), axis=1, keepdims=True)
    root = lax.rsqrt(variance * share / N_ALL + EPS)
    for copy in pieces:
        copy.wait()
    for d in range(3):
        total += part_in[d].astype(jnp.float32)
    out_ref[...] = total * root


def score(samples, sizes, phenotype, blocks, dosages):
    vmem = pl.BlockSpec(memory_space=pltpu.VMEM)
    smem = pl.BlockSpec(memory_space=pltpu.SMEM)
    hbm = pl.BlockSpec(memory_space=pltpu.HBM)
    dma = pltpu.SemaphoreType.DMA
    n_sends = sum(len(forwards(p, a, b)) for _, p, a, b in GATHER)
    return pl.pallas_call(
        scores_kernel,
        name="scores",
        out_shape=jax.ShapeDtypeStruct((32, M), jnp.float32),
        in_specs=[smem, hbm, hbm, hbm, hbm],
        out_specs=vmem,
        scratch_shapes=[
            pltpu.SMEM((NBINS * B,), jnp.int32),
            pltpu.VMEM((B, T), jnp.bfloat16),
            pltpu.VMEM((1, B, B), jnp.float32),
            pltpu.VMEM((N, 8, 128), jnp.float32),
            pltpu.VMEM((NBINS * B, M), jnp.bfloat16),
            pltpu.VMEM((NBINS, MSG, B), jnp.bfloat16),
            pltpu.VMEM((T, M), jnp.float32),
            pltpu.VMEM((16, M), jnp.float32),
            pltpu.VMEM((16, T), jnp.float32),
            pltpu.VMEM((4, 32, M), jnp.bfloat16),
            pltpu.VMEM((4, 32, M), jnp.bfloat16),
            pltpu.VMEM((3, 32, M), jnp.bfloat16),
            pltpu.VMEM((3, 32, M), jnp.bfloat16),
            pltpu.VMEM((2, 1, TS), jnp.float32),
            pltpu.VMEM((4, 1, TS), jnp.float32),
            dma((n_sends,)), dma((2, NBINS)), dma((LOADS,)), dma((3,)),
            dma((4,)), dma((4,)), dma((3,)), dma((3,)), dma((4,)), dma((4,)),
        ],
        compiler_params=pltpu.CompilerParams(
            collective_id=0, has_side_effects=True, vmem_limit_bytes=52 << 20
        ),
    )(sizes, samples, phenotype, blocks, dosages)


def local(phenotype, inverse_blocks, bin_sizes, slot_of, dosages):
    samples = invert(slot_of).reshape(NBINS * B)
    return score(samples, bin_sizes, phenotype, inverse_blocks, dosages).T


def solution(mesh):
    split = Mesh(mesh.devices.reshape(NX, 2, NZ, NY), (X, CORE, Z, Y))
    samp, var, both = (X, CORE), (Z, Y), (X, CORE, Z, Y)
    in_specs = (P(both, None), P(both, None, None), P(samp, var), P(samp), P(samp, var))
    return jax.shard_map(local, mesh=split, in_specs=in_specs, out_specs=P(var, samp), check_vma=False)
```
